1024 devices in a mesh: row: 8 (over y_hi, core), src: 128 (over z, y_lo, x).
Axes of the slice: x: 8, y: 8 (y_hi: 4, y_lo: 2; y = y_hi * 2 + y_lo), z: 8, core: 2. Of those that a mesh axis runs over, the one named last changes fastest.
Arguments:
- front_panel: float32 [3, 256, 16384], P(None, None, ('row', 'src')), may hold values from -0.046875 to 0.046875
- solved_prev: float32 [16384, 32768], P('row', 'src'), may hold values from -6 to 6
- right_side: float32 [768, 32768], P(None, 'src'), may hold values from -6 to 6
- front_window: float32 [768, 768], replicated, may hold values from -0.21875 to 0.21875
- inv_diag: float32 [3, 256, 256], replicated, may hold values from -0.375 to 0.375
- owner_map: int32 [3], replicated, may hold values from 0 to 7, as said below
Outputs:
- stored: float32 [2048, 32768], P('row', 'src')
The draws below stay inside these ranges and needn't reach their ends.
Inputs may be any that keep to these rules, and one draw needn't show every extreme that they name: `owner_map`: the blocks' owners are distinct row groups.
All inputs are finite; a program needn't handle non-finite values.
Results may differ from the reference program's by a relative error of at most 0.0001.
Values sent between devices are 32-bit elements; how exact they have to be, the bound alone decides.
No kernel may reach another device: no remote copies, remote signals or barrier semaphores. Data moves between devices by JAX's collectives and lax.ppermute only.
A program may use at most 64 MiB of HBM per device.

```python
import jax
import jax.numpy as jnp
from jax import lax

NB = 256
NBLK = 3
WIN = 768
PREV = 16384
SOURCES = 32768
N_ROW = 8


def draw_owner_map(key, part):
    middle = jax.random.permutation(jax.random.fold_in(key, 7), N_ROW - 2).astype(jnp.int32) + 1
    ends = jnp.array([0, N_ROW - 1], jnp.int32)
    chosen = jnp.concatenate([ends, middle[:NBLK - 2]])
    return jax.random.permutation(jax.random.fold_in(key, 11), chosen).astype(jnp.int32)


def steps_of(rng, shape, cuts, smallest, high):
    gain, own = 1.0, jax.random.fold_in(rng, 6)
    for dim, shards_of in cuts:
        heights = jnp.exp(jax.random.uniform(jax.random.fold_in(own, dim), (shards_of,), jnp.float32, smallest / len(cuts), high / len(cuts)))
        gain = gain * jnp.repeat(heights, shape[dim] // shards_of).reshape([-1 if axis == dim else 1 for axis in range(len(shape))])
    return gain


def normal_values(key, extent, scale, limit, cuts=(), kind=jnp.bfloat16):
    drawn = jax.random.normal(key, extent, jnp.float32) * scale
    if len(cuts) > 0:
        drawn = steps_of(key, extent, cuts, -0.22, 0.18) * drawn
    return jnp.clip(drawn, min=-limit, max=limit).astype(kind)


def setup_inputs(seed: int = 0) -> dict:
    arg_keys = jax.random.split(jax.random.key(seed), 7)
    front_panel = normal_values(arg_keys[0], (NBLK, NB, PREV), PREV ** -0.5, 0.046875, ((2, 1024),), jnp.float32)
    solved_prev = normal_values(arg_keys[1], (PREV, SOURCES), 1.0, 6.0, ((0, 8), (1, 128)), jnp.float32)
    right_side = normal_values(arg_keys[2], (WIN, SOURCES), 1.0, 6.0, ((1, 128),), jnp.float32)
    front_window = normal_values(arg_keys[3], (WIN, WIN), WIN ** -0.5, 0.21875, (), jnp.float32)
    inv_diag = normal_values(arg_keys[4], (NBLK, NB, NB), NB ** -0.5, 0.375, (), jnp.float32)
    owner_map = draw_owner_map(jax.random.fold_in(arg_keys[6], 71), 0)
    return dict(front_panel=front_panel, solved_prev=solved_prev, right_side=right_side, front_window=front_window, inv_diag=inv_diag, owner_map=owner_map)


def reference(front_panel, solved_prev, right_side, front_window, inv_diag, owner_map):
    highest = lax.Precision.HIGHEST
    stored = jnp.zeros((N_ROW * NB, right_side.shape[1]), jnp.float32)
    solutions = []
    for k in range(NBLK):
        partial_value = jnp.dot(front_panel[k], solved_prev, precision=highest, preferred_element_type=jnp.float32)
        rhs = right_side[k * NB:(k + 1) * NB] - partial_value
        if k > 0:
            earlier = jnp.concatenate(solutions, axis=0)
            rhs = rhs - jnp.dot(front_window[k * NB:(k + 1) * NB, :k * NB], earlier, precision=highest, preferred_element_type=jnp.float32)
        solution = jnp.dot(inv_diag[k], rhs, precision=highest, preferred_element_type=jnp.float32)
        solutions.append(solution)
        start = (owner_map[k] * NB).astype(jnp.int32)
        stored = lax.dynamic_update_slice(stored, solution, (start, jnp.int32(0)))
    return stored
```

```python
import jax
import jax.numpy as jnp
from jax import lax
from jax.sharding import Mesh
from jax.sharding import PartitionSpec as P

SRC = ("src_0", "src_1", "src_2")
ROW_SRC = ("row", "src_0", "src_1", "src_2")
HIGH = lax.Precision.HIGH
HIGHEST = lax.Precision.HIGHEST


def dot(a, b, dims, precision):
    return lax.dot_general(
        a, b, (dims, ((), ())), precision=precision, preferred_element_type=jnp.float32
    )


def passed_on(value, axis, step):
    n = lax.axis_size(axis)
    return lax.ppermute(value, axis, [(i, (i + step) % n) for i in range(n)])


def ring(block, axis):
    n = lax.axis_size(axis)
    half = block.shape[0] // 2
    up = down = block
    yield 0, 0, block
    for step in range(1, n // 2):
        up, down = passed_on(up, axis, 1), passed_on(down, axis, -1)
        yield -step, 0, up
        yield step, 0, down
    yield n // 2, 0, passed_on(up[:half], axis, 1)
    yield n // 2, half, passed_on(down[half:], axis, -1)


def gathered(block, axis):
    n = lax.axis_size(axis)
    parts = {}
    for offset, first, rows in ring(block, axis):
        parts[offset % n, first] = rows
    return jnp.concatenate([parts[key] for key in sorted(parts)], axis=0)


def turned(x, axis_name, dim):
    n = x.shape[dim]
    return lax.dynamic_slice_in_dim(
        jnp.concatenate([x, x], axis=dim), lax.axis_index(axis_name), n, axis=dim
    )


def body(front_panel, solved_prev, right_side, front_window, inv_diag, owner_map):
    nblk, block, own = front_panel.shape
    prev, width = solved_prev.shape
    groups = lax.axis_size("row")
    part = width // groups
    here = lax.axis_index("row")
    n0, n1, n2 = (lax.axis_size(axis) for axis in SRC)

    mine = front_panel.transpose(2, 0, 1).reshape(own, nblk * block)
    theirs = passed_on(mine, "src_1", 1)

    rows_of = solved_prev.reshape(n0, n1, n2, own, width)
    y = lax.axis_index("src_1")
    near = lax.dynamic_index_in_dim(rows_of, y, 1, keepdims=False)
    far = lax.dynamic_index_in_dim(rows_of, n1 - 1 - y, 1, keepdims=False)
    near = turned(near, "src_2", 1).transpose(0, 3, 1, 2).reshape(n0, width, n2 * own)
    far = turned(far, "src_0", 0).transpose(1, 3, 0, 2).reshape(n2, width, n0 * own)
    sides = lax.dynamic_slice_in_dim(right_side, here * part, part, axis=1).T

    local = jnp.zeros((width, nblk * block), jnp.float32)
    rings = zip(
        ring(gathered(mine, "src_2"), "src_0"),
        ring(gathered(theirs, "src_0"), "src_2"),
    )
    for pair in rings:
        for (offset, first, rows), held, axis in zip(pair, (near, far), ("src_0", "src_2")):
            n = lax.axis_size(axis)
            columns = lax.dynamic_index_in_dim(
                held, (lax.axis_index(axis) + offset) % n, 0, keepdims=False
            )
            local += dot(columns[:, first : first + rows.shape[0]], rows, ((1,), (0,)), HIGH)
    pieces = lax.all_to_all(local.reshape(groups, part, nblk * block), "row", 0, 0, tiled=True)
    rest = sides - pieces.sum(axis=0)
    routed = jnp.zeros((groups, part, block), jnp.float32)
    solutions = []
    slots = jnp.arange(groups, dtype=owner_map.dtype)[:, None, None]
    for k in range(nblk):
        rhs = rest[:, k * block : (k + 1) * block]
        for j, earlier in enumerate(solutions):
            window = front_window[k * block : (k + 1) * block, j * block : (j + 1) * block]
            rhs = rhs - dot(earlier, window, ((1,), (1,)), HIGHEST)
        solution_k = dot(rhs, inv_diag[k], ((1,), (1,)), HIGHEST)
        solutions.append(solution_k)
        routed = jnp.where(slots == owner_map[k], solution_k[None], routed)
    arrived = lax.all_to_all(routed, "row", 0, 0, tiled=True)
    return arrived.reshape(width, block).T


def solution(mesh):
    split = Mesh(
        mesh.devices.reshape(mesh.shape["row"], 8, 2, 8), ("row", "src_0", "src_1", "src_2")
    )
    return jax.shard_map(
        body,
        mesh=split,
        in_specs=(P(None, None, ROW_SRC), P("row", SRC), P(None, SRC), P(), P(), P()),
        out_specs=P("row", SRC),
        check_vma=False,
    )
```

```python
import jax
import jax.numpy as jnp
from jax import lax
from jax.sharding import Mesh
from jax.sharding import PartitionSpec as P


ROW = ("y_hi", "core")
SRC = ("z", "y_lo", "x")
HIGH = lax.Precision.HIGH
HIGHEST = lax.Precision.HIGHEST
CHUNKS = ((0, 2), (2, 3))


def dot(a, b, dims, precision):
    return lax.dot_general(
        a, b, (dims, ((), ())), precision=precision, preferred_element_type=jnp.float32
    )


def swapped(value, axis):
    return lax.ppermute(value, axis, [(0, 1), (1, 0)])


def in_order(mine, other, axis, dim):
    first = lax.axis_index(axis) == 0
    return jnp.stack([jnp.where(first, mine, other), jnp.where(first, other, mine)], axis=dim)


def body(front_panel, solved_prev, right_side, front_window, inv_diag, owner_map):
    nblk, block, own = front_panel.shape
    _, width = solved_prev.shape
    nz, ny, nx = (lax.axis_size(axis) for axis in SRC)
    nhi, ncore = (lax.axis_size(axis) for axis in ROW)
    groups = nhi * ncore
    part = width // groups
    here = lax.axis_index(ROW)
    y = lax.axis_index("y_lo")
    core = lax.axis_index("core")
    depth = nz * nx * own

    rows_of = solved_prev.reshape(nz, ny, nx * own, width)
    far = lax.dynamic_index_in_dim(rows_of, ny - 1 - y, 1, keepdims=False)
    got = swapped(far, "y_lo")
    near = lax.dynamic_index_in_dim(rows_of, y, 1, keepdims=False)

    panel = front_panel.transpose(2, 0, 1).reshape(own, nblk * block)
    panels, column = [], None
    for first, last in CHUNKS:
        piece = panel[:, first * block : last * block]
        if column is not None:
            piece, column = lax.optimization_barrier((piece, column))
        copies = jnp.broadcast_to(piece[None], (nx, *piece.shape))
        column = lax.all_to_all(copies, "x", 0, 0, tiled=True)
        panels.append(lax.all_gather(column.reshape(nx * own, -1), "z", axis=0, tiled=True))

    sources = in_order(near, got, "y_lo", 0).reshape(ny, depth, width).transpose(0, 2, 1)
    sources = sources.reshape(ny, nhi, ncore, part, depth)
    kept, given = (
        lax.dynamic_index_in_dim(sources, which, 2, keepdims=False)
        .transpose(1, 0, 2, 3)
        .reshape(nhi * ny * part, depth)
        for which in (core, ncore - 1 - core)
    )
    sides = lax.dynamic_slice_in_dim(right_side, here * part, part, axis=1).T

    slots = jnp.arange(groups, dtype=owner_map.dtype)[:, None, None]
    routed = jnp.zeros((groups, part, block), jnp.float32)
    solutions = []
    for (first, last), gathered in zip(CHUNKS, panels):
        others = dot(given, gathered, ((1,), (0,)), HIGH)
        arrived = swapped(others, "core")
        local = lax.optimization_barrier(dot(kept, gathered, ((1,), (0,)), HIGH))
        local = local + arrived
        pieces = lax.all_to_all(
            local.reshape(nhi * ny, part, -1), ("y_hi", "y_lo"), 0, 0, tiled=True
        )
        rest = sides[:, first * block : last * block] - pieces.sum(axis=0)
        for k in range(first, last):
            rhs = rest[:, (k - first) * block : (k - first + 1) * block]
            for j, earlier in enumerate(solutions):
                window = front_window[k * block : (k + 1) * block, j * block : (j + 1) * block]
                rhs = rhs - dot(earlier, window, ((1,), (1,)), HIGHEST)
            solution_k = dot(rhs, inv_diag[k], ((1,), (1,)), HIGHEST)
            solutions.append(solution_k)
            routed = jnp.where(slots == owner_map[k], solution_k[None], routed)
    stored = lax.all_to_all(routed, ROW, 0, 0, tiled=True)
    return stored.reshape(width, block).T


def solution(mesh):
    split = Mesh(
        mesh.devices.reshape(mesh.shape["row"] // 2, 2, 8, 2, 8), ("y_hi", "core", "z", "y_lo", "x")
    )
    return jax.shard_map(
        body,
        mesh=split,
        in_specs=(P(None, None, (*ROW, *SRC)), P(ROW, SRC), P(None, SRC), P(), P(), P()),
        out_specs=P(ROW, SRC),
        check_vma=False,
    )
```

```python
import jax
import jax.numpy as jnp
from jax import lax
from jax.sharding import Mesh
from jax.sharding import PartitionSpec as P


ROW = ("y_hi", "core")
SRC = ("z", "y_lo", "x")
HIGH = lax.Precision.HIGH
HIGHEST = lax.Precision.HIGHEST


def dot(a, b, dims, precision):
    return lax.dot_general(
        a, b, (dims, ((), ())), precision=precision, preferred_element_type=jnp.float32
    )


def swapped(value, axis):
    return lax.ppermute(value, axis, [(0, 1), (1, 0)])


def passed_on(value, axis, step):
    n = lax.axis_size(axis)
    return lax.ppermute(value, axis, [(i, (i + step) % n) for i in range(n)])


def ring(rows, axis):
    n = lax.axis_size(axis)
    half = rows.shape[0] // 2
    up = down = rows
    yield 0, 0, rows
    for step in range(1, n // 2):
        up, down = passed_on(up, axis, 1), passed_on(down, axis, -1)
        yield -step, 0, up
        yield step, 0, down
    yield n // 2, 0, passed_on(up[:half], axis, 1)
    yield n // 2, half, passed_on(down[half:], axis, -1)


def in_order(mine, other, axis, dim):
    first = lax.axis_index(axis) == 0
    return jnp.stack([jnp.where(first, mine, other), jnp.where(first, other, mine)], axis=dim)


def body(front_panel, solved_prev, right_side, front_window, inv_diag, owner_map):
    nblk, block, own = front_panel.shape
    _, width = solved_prev.shape
    nz, ny, nx = (lax.axis_size(axis) for axis in SRC)
    nhi, ncore = (lax.axis_size(axis) for axis in ROW)
    groups = nhi * ncore
    part = width // groups
    here = lax.axis_index(ROW)
    y = lax.axis_index("y_lo")
    core = lax.axis_index("core")

    rows_of = solved_prev.reshape(nz, ny, nx * own, width)
    far = lax.dynamic_index_in_dim(rows_of, ny - 1 - y, 1, keepdims=False)
    got = swapped(far, "y_lo")
    near = lax.dynamic_index_in_dim(rows_of, y, 1, keepdims=False)

    panel = front_panel.transpose(2, 0, 1).reshape(own, nblk * block)
    column = lax.all_to_all(
        jnp.broadcast_to(panel[None], (nx, *panel.shape)), "x", 0, 0, tiled=True
    )
    column = column.reshape(nx * own, nblk * block)

    sources = in_order(near, got, "y_lo", 0).reshape(ny, nz, nx * own, width).transpose(1, 0, 3, 2)
    sources = sources.reshape(nz, ny, nhi, ncore, part, nx * own)
    kept, given = (
        lax.dynamic_index_in_dim(sources, which, 3, keepdims=False)
        .transpose(0, 2, 1, 3, 4)
        .reshape(nz, nhi * ny * part, nx * own)
        for which in (core, ncore - 1 - core)
    )
    sides = lax.dynamic_slice_in_dim(right_side, here * part, part, axis=1).T

    local = jnp.zeros((nhi * ny * part, nblk * block), jnp.float32)
    others = local
    for offset, first, rows in ring(column, "z"):
        place = (lax.axis_index("z") + offset) % nz
        span = slice(first, first + rows.shape[0])
        given_rows, kept_rows = (
            lax.dynamic_index_in_dim(held, place, 0, keepdims=False)[:, span]
            for held in (given, kept)
        )
        others += dot(given_rows, rows, ((1,), (0,)), HIGH)
        local += dot(kept_rows, rows, ((1,), (0,)), HIGH)
    local = lax.optimization_barrier(local) + swapped(others, "core")
    pieces = lax.all_to_all(
        local.reshape(nhi * ny, part, nblk * block), ("y_hi", "y_lo"), 0, 0, tiled=True
    )
    rest = sides - pieces.sum(axis=0)

    slots = jnp.arange(groups, dtype=owner_map.dtype)[:, None, None]
    routed = jnp.zeros((groups, part, block), jnp.float32)
    solutions = []
    for k in range(nblk):
        rhs = rest[:, k * block : (k + 1) * block]
        for j, earlier in enumerate(solutions):
            window = front_window[k * block : (k + 1) * block, j * block : (j + 1) * block]
            rhs = rhs - dot(earlier, window, ((1,), (1,)), HIGHEST)
        solution_k = dot(rhs, inv_diag[k], ((1,), (1,)), HIGHEST)
        solutions.append(solution_k)
        routed = jnp.where(slots == owner_map[k], solution_k[None], routed)
    stored = lax.all_to_all(routed, ROW, 0, 0, tiled=True)
    return stored.reshape(width, block).T


def solution(mesh):
    split = Mesh(
        mesh.devices.reshape(mesh.shape["row"] // 2, 2, 8, 2, 8), ("y_hi", "core", "z", "y_lo", "x")
    )
    return jax.shard_map(
        body,
        mesh=split,
        in_specs=(P(None, None, (*ROW, *SRC)), P(ROW, SRC), P(None, SRC), P(), P(), P()),
        out_specs=P(ROW, SRC),
        check_vma=False,
    )
```

```python
import jax
import jax.numpy as jnp
from jax import lax
from jax.sharding import Mesh
from jax.sharding import PartitionSpec as P


ROW = ("y_hi", "core")
SRC = ("z", "y_lo", "x")
HIGH = lax.Precision.HIGH
HIGHEST = lax.Precision.HIGHEST


def dot(a, b, dims, precision):
    return lax.dot_general(
        a, b, (dims, ((), ())), precision=precision, preferred_element_type=jnp.float32
    )


def swapped(value, axis):
    return lax.ppermute(value, axis, [(0, 1), (1, 0)])


def passed_on(value, axis, step):
    n = lax.axis_size(axis)
    return lax.ppermute(value, axis, [(i, (i + step) % n) for i in range(n)])


def ring(rows, axis):
    n = lax.axis_size(axis)
    half = rows.shape[0] // 2
    up = down = rows
    yield 0, 0, rows
    for step in range(1, n // 2):
        up, down = passed_on(up, axis, 1), passed_on(down, axis, -1)
        yield -step, 0, up
        yield step, 0, down
    yield n // 2, 0, passed_on(up[:half], axis, 1)
    yield n // 2, half, passed_on(down[half:], axis, -1)


def body(front_panel, solved_prev, right_side, front_window, inv_diag, owner_map):
    nblk, block, own = front_panel.shape
    _, width = solved_prev.shape
    nz, ny, nx = (lax.axis_size(axis) for axis in SRC)
    nhi, ncore = (lax.axis_size(axis) for axis in ROW)
    groups = nhi * ncore
    part = width // groups
    here = lax.axis_index(ROW)
    y = lax.axis_index("y_lo")
    core = lax.axis_index("core")

    rows_of = solved_prev.reshape(nz, ny, nx * own, width)
    far = lax.dynamic_index_in_dim(rows_of, ny - 1 - y, 1, keepdims=False)
    got = swapped(far, "y_lo")
    near = lax.dynamic_index_in_dim(rows_of, y, 1, keepdims=False)

    panel = front_panel.transpose(2, 0, 1).reshape(own, nblk * block)
    column = lax.all_to_all(
        jnp.broadcast_to(panel[None], (nx, *panel.shape)), "x", 0, 0, tiled=True
    )
    column = column.reshape(nx * own, nblk * block)

    sources = jnp.stack([near, got]).reshape(ny, nz, nx * own, width).transpose(1, 0, 3, 2)
    sources = sources.reshape(nz, ny, nhi, ncore, part, nx * own)
    kept, given = (
        lax.dynamic_index_in_dim(sources, which, 3, keepdims=False).reshape(
            nz, ny * nhi * part, nx * own
        )
        for which in (core, ncore - 1 - core)
    )
    sides = lax.dynamic_slice_in_dim(right_side, here * part, part, axis=1).T

    local = jnp.zeros((ny * nhi * part, nblk * block), jnp.float32)
    others = local
    for offset, first, rows in ring(column, "z"):
        place = (lax.axis_index("z") + offset) % nz
        span = slice(first, first + rows.shape[0])
        given_rows, kept_rows = (
            lax.dynamic_index_in_dim(held, place, 0, keepdims=False)[:, span]
            for held in (given, kept)
        )
        others += dot(given_rows, rows, ((1,), (0,)), HIGH)
        local += dot(kept_rows, rows, ((1,), (0,)), HIGH)
    local = lax.optimization_barrier(local) + swapped(others, "core")
    local = local.reshape(ny, nhi, part, nblk * block)
    local = local[0] + swapped(local[1], "y_lo")
    pieces = lax.all_to_all(local, "y_hi", 0, 0, tiled=True)
    rest = sides - pieces.sum(axis=0)

    slots = jnp.arange(groups, dtype=owner_map.dtype)[:, None, None]
    routed = jnp.zeros((groups, part, block), jnp.float32)
    solutions = []
    for k in range(nblk):
        rhs = rest[:, k * block : (k + 1) * block]
        for j, earlier in enumerate(solutions):
            window = front_window[k * block : (k + 1) * block, j * block : (j + 1) * block]
            rhs = rhs - dot(earlier, window, ((1,), (1,)), HIGHEST)
        solution_k = dot(rhs, inv_diag[k], ((1,), (1,)), HIGHEST)
        solutions.append(solution_k)
        routed = jnp.where(slots == owner_map[k], solution_k[None], routed)
    stored = lax.all_to_all(routed, ROW, 0, 0, tiled=True)
    return stored.reshape(width, block).T


def solution(mesh):
    split = Mesh(
        mesh.devices.reshape(mesh.shape["row"] // 2, 2, 8, 2, 8), ("y_hi", "core", "z", "y_lo", "x")
    )
    return jax.shard_map(
        body,
        mesh=split,
        in_specs=(P(None, None, (*ROW, *SRC)), P(ROW, SRC), P(None, SRC), P(), P(), P()),
        out_specs=P(ROW, SRC),
        check_vma=False,
    )
```

```python
import jax
import jax.numpy as jnp
from jax import lax
from jax.sharding import Mesh
from jax.sharding import PartitionSpec as P


ROW = ("y_hi", "core")
SRC = ("z", "y_lo", "x")
HIGH = lax.Precision.HIGH
HIGHEST = lax.Precision.HIGHEST


def dot(a, b, dims, precision):
    return lax.dot_general(
        a, b, (dims, ((), ())), precision=precision, preferred_element_type=jnp.float32
    )


def swapped(value, axis):
    return lax.ppermute(value, axis, [(0, 1), (1, 0)])


def passed_on(value, axis, step):
    n = lax.axis_size(axis)
    return lax.ppermute(value, axis, [(i, (i + step) % n) for i in range(n)])


def ring(rows, axis):
    n = lax.axis_size(axis)
    half = rows.shape[0] // 2
    up = down = rows
    yield 0, 0, rows
    for step in range(1, n // 2):
        up, down = passed_on(up, axis, 1), passed_on(down, axis, -1)
        yield -step, 0, up
        yield step, 0, down
    yield n // 2, 0, passed_on(up[:half], axis, 1)
    yield n // 2, half, passed_on(down[half:], axis, -1)


def in_order(mine, other, axis, dim):
    first = lax.axis_index(axis) == 0
    return jnp.stack([jnp.where(first, mine, other), jnp.where(first, other, mine)], axis=dim)


def solve_operator(front_window, inv_diag):
    nblk, block, _ = inv_diag.shape
    rows = inv_diag[0]
    for k in range(1, nblk):
        window = front_window[k * block : (k + 1) * block, : k * block]
        before = dot(window, rows, ((1,), (0,)), HIGHEST)
        below = -dot(inv_diag[k], before, ((1,), (0,)), HIGHEST)
        rows = jnp.concatenate(
            [
                jnp.pad(rows, ((0, 0), (0, block))),
                jnp.concatenate([below, inv_diag[k]], axis=1),
            ],
            axis=0,
        )
    return rows


def body(front_panel, solved_prev, right_side, front_window, inv_diag, owner_map):
    nblk, block, own = front_panel.shape
    _, width = solved_prev.shape
    nz, ny, nx = (lax.axis_size(axis) for axis in SRC)
    nhi, ncore = (lax.axis_size(axis) for axis in ROW)
    groups = nhi * ncore
    part = width // groups
    here = lax.axis_index(ROW)
    y = lax.axis_index("y_lo")
    core = lax.axis_index("core")

    rows_of = solved_prev.reshape(nz, ny, nx * own, width)
    far = lax.dynamic_index_in_dim(rows_of, ny - 1 - y, 1, keepdims=False)
    got = swapped(far, "y_lo")
    near = lax.dynamic_index_in_dim(rows_of, y, 1, keepdims=False)

    panel = front_panel.transpose(2, 0, 1).reshape(own, nblk * block)
    column = lax.all_to_all(
        jnp.broadcast_to(panel[None], (nx, *panel.shape)), "x", 0, 0, tiled=True
    )
    column = column.reshape(nx * own, nblk * block)

    sources = in_order(near, got, "y_lo", 0).reshape(ny, nz, nx * own, width).transpose(1, 0, 3, 2)
    sources = sources.reshape(nz, ny, nhi, ncore, part, nx * own)
    kept, given = (
        lax.dynamic_index_in_dim(sources, which, 3, keepdims=False)
        .transpose(0, 2, 1, 3, 4)
        .reshape(nz, nhi * ny * part, nx * own)
        for which in (core, ncore - 1 - core)
    )
    sides = lax.dynamic_slice_in_dim(right_side, here * part, part, axis=1).T

    local = jnp.zeros((nhi * ny * part, nblk * block), jnp.float32)
    others = local
    for offset, first, rows in ring(column, "z"):
        place = (lax.axis_index("z") + offset) % nz
        span = slice(first, first + rows.shape[0])
        given_rows, kept_rows = (
            lax.dynamic_index_in_dim(held, place, 0, keepdims=False)[:, span]
            for held in (given, kept)
        )
        others += dot(given_rows, rows, ((1,), (0,)), HIGH)
        local += dot(kept_rows, rows, ((1,), (0,)), HIGH)
    local = lax.optimization_barrier(local) + swapped(others, "core")
    pieces = lax.all_to_all(
        local.reshape(nhi * ny, part, nblk * block), ("y_hi", "y_lo"), 0, 0, tiled=True
    )
    rest = sides - pieces.sum(axis=0)

    operator = lax.optimization_barrier(solve_operator(front_window, inv_diag))
    solved = dot(rest, operator, ((1,), (1,)), HIGHEST)
    slots = jnp.arange(groups, dtype=owner_map.dtype)[:, None, None]
    routed = jnp.zeros((groups, part, block), jnp.float32)
    for k in range(nblk):
        solution_k = solved[:, k * block : (k + 1) * block]
        routed = jnp.where(slots == owner_map[k], solution_k[None], routed)
    stored = lax.all_to_all(routed, ROW, 0, 0, tiled=True)
    return stored.reshape(width, block).T


def solution(mesh):
    split = Mesh(
        mesh.devices.reshape(mesh.shape["row"] // 2, 2, 8, 2, 8), ("y_hi", "core", "z", "y_lo", "x")
    )
    return jax.shard_map(
        body,
        mesh=split,
        in_specs=(P(None, None, (*ROW, *SRC)), P(ROW, SRC), P(None, SRC), P(), P(), P()),
        out_specs=P(ROW, SRC),
        check_vma=False,
    )
```

```python
import jax
import jax.numpy as jnp
from jax import lax
from jax.sharding import Mesh
from jax.sharding import PartitionSpec as P


ROW = ("y_hi", "core")
SRC = ("z", "y_lo", "x")
HIGH = lax.Precision.HIGH
HIGHEST = lax.Precision.HIGHEST


def dot(a, b, dims, precision):
    return lax.dot_general(
        a, b, (dims, ((), ())), precision=precision, preferred_element_type=jnp.float32
    )


def swapped(value, axis):
    return lax.ppermute(value, axis, [(0, 1), (1, 0)])


def passed_on(value, axis, step):
    n = lax.axis_size(axis)
    return lax.ppermute(value, axis, [(i, (i + step) % n) for i in range(n)])


def ring(rows, axis):
    n = lax.axis_size(axis)
    half = rows.shape[0] // 2
    up = down = rows
    yield 0, 0, rows
    for step in range(1, n // 2):
        up = passed_on(up, axis, 1)
        down = passed_on(down, axis, -1)
        yield -step, 0, up
        yield step, 0, down
    yield n // 2, 0, passed_on(up[:half], axis, 1)
    yield n // 2, half, passed_on(down[half:], axis, -1)


def in_order(mine, other, axis, dim):
    first = lax.axis_index(axis) == 0
    return jnp.stack([jnp.where(first, mine, other), jnp.where(first, other, mine)], axis=dim)


def solve_operator(front_window, inv_diag):
    nblk, block, _ = inv_diag.shape
    rows = inv_diag[0]
    for k in range(1, nblk):
        window = front_window[k * block : (k + 1) * block, : k * block]
        before = dot(window, rows, ((1,), (0,)), HIGHEST)
        below = -dot(inv_diag[k], before, ((1,), (0,)), HIGHEST)
        rows = jnp.concatenate(
            [
                jnp.pad(rows, ((0, 0), (0, block))),
                jnp.concatenate([below, inv_diag[k]], axis=1),
            ],
            axis=0,
        )
    return rows


def body(front_panel, solved_prev, right_side, front_window, inv_diag, owner_map):
    nblk, block, own = front_panel.shape
    _, width = solved_prev.shape
    nz, ny, nx = (lax.axis_size(axis) for axis in SRC)
    nhi, ncore = (lax.axis_size(axis) for axis in ROW)
    groups = nhi * ncore
    part = width // groups
    here = lax.axis_index(ROW)
    y = lax.axis_index("y_lo")
    core = lax.axis_index("core")

    rows_of = solved_prev.reshape(nz, ny, nx * own, width)
    far = lax.dynamic_index_in_dim(rows_of, ny - 1 - y, 1, keepdims=False)
    got = swapped(far, "y_lo")
    near = lax.dynamic_index_in_dim(rows_of, y, 1, keepdims=False)

    panel = front_panel.transpose(2, 0, 1).reshape(own, nblk * block)
    column = lax.all_to_all(
        jnp.broadcast_to(panel[None], (nx, *panel.shape)), "x", 0, 0, tiled=True
    )
    column = column.reshape(nx * own, nblk * block)

    sources = in_order(near, got, "y_lo", 0)
    sources = sources.reshape(ny, nz, nx * own, width).transpose(1, 0, 3, 2)
    sources = sources.reshape(nz, ny, nhi, ncore, part, nx * own)
    kept, given = (
        lax.dynamic_index_in_dim(sources, which, 3, keepdims=False)
        .transpose(0, 2, 1, 3, 4)
        .reshape(nz, nhi * ny * part, nx * own)
        for which in (core, ncore - 1 - core)
    )
    sides = lax.dynamic_slice_in_dim(right_side, here * part, part, axis=1).T

    local = jnp.zeros((nhi * ny * part, nblk * block), jnp.float32)
    others = local
    for offset, first, rows in ring(column, "z"):
        place = (lax.axis_index("z") + offset) % nz
        span = slice(first, first + rows.shape[0])
        given_rows, kept_rows = (
            lax.dynamic_index_in_dim(held, place, 0, keepdims=False)[:, span]
            for held in (given, kept)
        )
        others += dot(given_rows, rows, ((1,), (0,)), HIGH)
        local += dot(kept_rows, rows, ((1,), (0,)), HIGH)
    local = lax.optimization_barrier(local) + swapped(others, "core")
    pieces = lax.all_to_all(
        local.reshape(nhi * ny, part, nblk * block), ("y_hi", "y_lo"), 0, 0, tiled=True
    )
    rest = sides - pieces.sum(axis=0)

    operator = lax.optimization_barrier(solve_operator(front_window, inv_diag))
    solved = dot(rest, operator, ((1,), (1,)), HIGHEST)
    slots = jnp.arange(groups, dtype=owner_map.dtype)[:, None, None]
    routed = jnp.zeros((groups, part, block), jnp.float32)
    for k in range(nblk):
        solution_k = solved[:, k * block : (k + 1) * block]
        routed = jnp.where(slots == owner_map[k], solution_k[None], routed)
    stored = lax.all_to_all(routed, ROW, 0, 0, tiled=True)
    return stored.reshape(width, block).T


def solution(mesh):
    split = Mesh(
        mesh.devices.reshape(mesh.shape["row"] // 2, 2, 8, 2, 8), ("y_hi", "core", "z", "y_lo", "x")
    )
    return jax.shard_map(
        body,
        mesh=split,
        in_specs=(P(None, None, (*ROW, *SRC)), P(ROW, SRC), P(None, SRC), P(), P(), P()),
        out_specs=P(ROW, SRC),
        check_vma=False,
    )
```
